128 devices in a mesh: chan: 32 (over x_lo, y, z), beam: 4 (over x_hi, core).
Axes of the slice: x: 4 (x_hi: 2, x_lo: 2; x = x_hi * 2 + x_lo), y: 4, z: 4, core: 2. Of those that a mesh axis runs over, the one named last changes fastest.
Arguments:
- samples: bfloat16 [32, 4096, 1024], P('beam', 'chan'), parts along dimension 0, may hold values from -6 to 6
- trial_steps: int32 [1024], P('chan'), may hold values from 0 to 1023
- chan_delay: int32 [4096], P('chan'), may hold values from 0 to 1023
Outputs:
- series: float32 [32, 1024, 128], P('beam', 'chan'), parts along dimension 0
The draws below stay inside these ranges and needn't reach their ends.
There are 4 independent parts, one for each index of `beam`. The reference program is written for one: setup_inputs(seed, part) draws one part's arguments, and reference() takes and returns one part's arrays. A program takes and returns all parts, laid end to end along the dimension named above; an argument that names none is the same for every part. Nothing has to cross between parts.
All inputs are finite; a program needn't handle non-finite values.
Results may differ from the reference program's by a relative error of at most 0.0056.
Values may be sent and summed in bfloat16 or wider, within the bound.
A program may use at most 128 MiB of HBM per device.

```python
import math
import jax
import jax.numpy as jnp
from jax import lax

BEAMS = 8
CHANNELS = 4096
SAMPLES = 1024
BINS = 32
TRIALS = 1024
OUT_SAMPLES = 128


def place_ends(result, own_key, low, high):
    dims = result.shape
    place = [jax.random.randint(jax.random.fold_in(own_key, axis), (), 0, dims[axis]) for axis in range(len(dims))]
    result = result.at[tuple(place)].set(low)
    longest = dims.index(max(dims))
    place[longest] = (place[longest] + 1) % dims[longest]
    return result.at[tuple(place)].set(high)


def block_levels(stream_key, extent, cuts, low, top_value):
    def one(position, shards_of):
        draws = jax.random.uniform(jax.random.fold_in(jax.random.fold_in(stream_key, 6), position), (shards_of,), jnp.float32, low / len(cuts), top_value / len(cuts))
        return jnp.repeat(jnp.exp(draws), extent[position] // shards_of).reshape((-1,) + (1,) * (len(extent) - position - 1))

    factor_of = one(*cuts[0])
    for cut in cuts[1:]:
        factor_of = factor_of * one(*cut)
    return factor_of


def scatter_about(stream_key, extent, spread, most, shards=(), kind=jnp.bfloat16):
    factor_of = block_levels(stream_key, extent, shards, -0.22, 0.18) if shards else 1.0
    result = jax.random.normal(stream_key, extent, jnp.float32) * spread * factor_of
    return jnp.minimum(jnp.maximum(result, -most), most).astype(kind)


def setup_inputs(seed: int = 0, part: int = 0) -> dict:
    streams_of = jax.random.split(jax.random.key(seed), 4)
    own_keys = jax.random.split(jax.random.fold_in(streams_of[3], part), 4)
    samples = scatter_about(own_keys[0], (BEAMS, CHANNELS, SAMPLES), 1.0, 6.0, ((1, 32),))
    trial_steps = place_ends(jax.random.randint(streams_of[1], (TRIALS,), 0, SAMPLES), jax.random.fold_in(streams_of[1], 1), 0, SAMPLES - 1).astype(jnp.int32)
    chan_delay = place_ends(jax.random.randint(streams_of[2], (CHANNELS,), 0, SAMPLES), jax.random.fold_in(streams_of[2], 1), 0, SAMPLES - 1).astype(jnp.int32)
    return {"samples": samples, "trial_steps": trial_steps, "chan_delay": chan_delay}


EPSILON = 1e-05

def turn_table(index_a, index_b, period):
    phase = index_a * index_b % period
    return phase.astype(jnp.float32) * (2.0 * math.pi / period)

def reference(samples, trial_steps, chan_delay):
    bin_index = jnp.arange(1, BINS + 1, dtype=jnp.int32)
    sample_index = jnp.arange(SAMPLES, dtype=jnp.int32)
    phase_angle = turn_table(bin_index[:, None], sample_index[None, :], SAMPLES)
    forward = jnp.concatenate([jnp.cos(phase_angle), -jnp.sin(phase_angle)], 0).astype(jnp.bfloat16)

    def spectrum(beam_rows):
        energy = lax.optimization_barrier(jnp.sum(jnp.square(beam_rows.astype(jnp.float32)), -1))
        scaling = 1.0 / jnp.sqrt(energy / SAMPLES + EPSILON) / math.sqrt(SAMPLES)
        product = jnp.dot(beam_rows, forward.T, preferred_element_type=jnp.float32)
        return (product * scaling[:, None]).astype(jnp.bfloat16)
    spectra = lax.map(spectrum, samples)
    real_in = spectra[:, :, :BINS]
    imag_in = spectra[:, :, BINS:]
    delay_steps = trial_steps[:, None] * chan_delay[None, :] % SAMPLES

    def one_bin(bin_number):
        angle_tab = turn_table(bin_number, delay_steps, SAMPLES)
        cos_tab = jnp.cos(angle_tab).astype(jnp.bfloat16)
        sin_tab = jnp.sin(angle_tab).astype(jnp.bfloat16)
        real_part_in = lax.dynamic_index_in_dim(real_in, bin_number - 1, 2, keepdims=False)
        imag_part_in = lax.dynamic_index_in_dim(imag_in, bin_number - 1, 2, keepdims=False)
        real_part = jnp.dot(real_part_in, cos_tab.T, preferred_element_type=jnp.float32) - jnp.dot(imag_part_in, sin_tab.T, preferred_element_type=jnp.float32)
        imag_part = jnp.dot(real_part_in, sin_tab.T, preferred_element_type=jnp.float32) + jnp.dot(imag_part_in, cos_tab.T, preferred_element_type=jnp.float32)
        return (jnp.stack([real_part, imag_part]) / math.sqrt(CHANNELS)).astype(jnp.bfloat16)
    dedispersed = lax.map(one_bin, bin_index)
    out_index = jnp.arange(OUT_SAMPLES, dtype=jnp.int32)
    back_angle = turn_table(bin_index[:, None], out_index[None, :], OUT_SAMPLES)
    backward = jnp.stack([jnp.cos(back_angle), -jnp.sin(back_angle)]).astype(jnp.bfloat16)
    series = jnp.einsum('krbd,rkt->bdt', dedispersed.astype(jnp.float32), backward.astype(jnp.float32), precision=lax.Precision.HIGHEST)
    return series / math.sqrt(BINS)
```

```python
import math

import jax
import jax.numpy as jnp
import numpy as np
from jax import lax
from jax.experimental import pallas as pl
from jax.experimental.pallas import tpu as pltpu
from jax.sharding import PartitionSpec as P

CHANNELS = 4096
SAMPLES = 1024
BINS = 32
TRIALS = 1024
OUT_SAMPLES = 128
EPSILON = 1e-05

GROUPS = 32
BEAMS = 8
CHAN_DEV = CHANNELS // GROUPS
TRIAL_DEV = TRIALS // GROUPS
LOW = 256
QUARTERS = SAMPLES // LOW
SIDES = (2, 4, 4)


def hops(offset):
    return sum(min(d, n - d) for d, n in zip(offset, SIDES))


OFFSETS = sorted(
    [(x, y, z) for x in range(2) for y in range(4) for z in range(4) if (x, y, z) != (0, 0, 0)],
    key=lambda offset: -hops(offset),
)


def turn(phase, period):
    return (phase % period).astype(np.float32) * np.float32(2.0 * math.pi / period)


def tables():
    bins = np.arange(1, BINS + 1)
    angle = turn(bins[:, None] * np.arange(SAMPLES)[None, :], SAMPLES)
    forward = np.concatenate([np.cos(angle), -np.sin(angle)])
    low = np.arange(LOW)
    m = np.arange(QUARTERS)[:, None, None] + QUARTERS * low[None, None, :]
    angle = turn(m * low[None, :, None], SAMPLES)
    twiddle = np.concatenate([np.cos(angle), np.sin(angle)], 2)
    angle = turn(bins[:, None] * np.arange(OUT_SAMPLES)[None, :], OUT_SAMPLES)
    backward = np.stack([np.cos(angle), -np.sin(angle)])
    spread = np.zeros((2, BINS, 4, 4, OUT_SAMPLES), np.float32)
    for p in range(4):
        spread[:, :, p, p] = backward
    spread = spread.reshape(2, BINS * 4, 4 * OUT_SAMPLES)
    return [jnp.asarray(t, jnp.bfloat16) for t in (forward, twiddle, spread)]


def dot_nt(a, b):
    return lax.dot_general(a, b, (((1,), (1,)), ((), ())), preferred_element_type=jnp.float32)


def kernel(
    samples_ref, steps_ref, delay_ref, forward_hbm, twiddle_hbm, spread_hbm, out_ref,
    samp, forward, twiddle, spread, tab, tabs, plain, send, recv, onehot, quarter, masked, pick,
    ded, ded_in, rows, in_sem, const_sem, tab_send, tab_recv, spec_send, spec_recv, ded_send, ded_recv,
):
    me = lax.axis_index("chan")
    mx, my, mz = me // 16, (me // 4) % 4, me % 4
    xs = [(mx + d) % 2 for d in range(2)]
    ys = [(my + d) % 4 for d in range(4)]
    zs = [(mz + d) % 4 for d in range(4)]
    peers = [xs[x] * 16 + ys[y] * 4 + zs[z] for x, y, z in OFFSETS]

    loads = [
        pltpu.make_async_copy(
            samples_ref.at[pl.ds(2 * i, 2)], samp.at[pl.ds(2 * i, 2)], in_sem.at[i]
        )
        for i in range(4)
    ]
    consts = [
        pltpu.make_async_copy(src, dst, const_sem.at[i])
        for i, (src, dst) in enumerate(
            ((forward_hbm, forward), (twiddle_hbm, twiddle), (spread_hbm, spread))
        )
    ]
    consts[0].start()
    for load in loads:
        load.start()
    consts[1].start()
    consts[2].start()

    barrier = pltpu.get_barrier_semaphore()
    for peer in peers:
        pl.semaphore_signal(
            barrier, inc=1, device_id={"chan": peer}, device_id_type=pl.DeviceIdType.MESH
        )

    steps = steps_ref[...]
    tab[0:1, :] = delay_ref[...]
    tab[1:2, :] = jnp.concatenate([steps] * (CHAN_DEV // TRIAL_DEV), axis=1)

    consts[0].wait()
    for i in range(4):
        loads[i].wait()
        block = samp[2 * i : 2 * i + 2].reshape(2 * CHAN_DEV, SAMPLES)
        product = dot_nt(forward[...], block)
        energy = jnp.zeros((2 * CHAN_DEV, 128), jnp.float32)
        for j in range(SAMPLES // 128):
            piece = block[:, 128 * j : 128 * (j + 1)].astype(jnp.float32)
            energy += piece * piece
        energy = jnp.sum(energy.T, axis=0, keepdims=True)
        scaling = 1.0 / jnp.sqrt(energy / SAMPLES + EPSILON) / math.sqrt(SAMPLES)
        product = product * scaling
        for half in range(2):
            for r in range(2):
                plain[pl.ds(r * BEAMS + 2 * i + half, BINS, stride=2 * BEAMS), :] = product[
                    r * BINS : (r + 1) * BINS, half * CHAN_DEV : (half + 1) * CHAN_DEV
                ]
    send[...] = plain[...].astype(jnp.bfloat16).reshape(BINS, 2 * BEAMS, CHAN_DEV)

    pl.semaphore_wait(barrier, GROUPS - 1)

    def exchange(pick_src, dst, send_sem, recv_sem):
        for n, peer in enumerate(peers):
            pltpu.make_async_remote_copy(
                src_ref=pick_src(peer),
                dst_ref=dst.at[me],
                send_sem=send_sem,
                recv_sem=recv_sem,
                device_id={"chan": peer},
                device_id_type=pl.DeviceIdType.MESH,
            ).start()

    def arrived(buffer, sem):
        part = buffer.at[pl.ds(0, GROUPS - 1)]
        pltpu.make_async_copy(part, part, sem).wait()

    exchange(lambda peer: tab, tabs, tab_send, tab_recv)
    exchange(lambda peer: send.at[peer], recv, spec_send, spec_recv)

    tabs[me] = tab[...]
    recv[me] = send[me]

    arrived(tabs, tab_recv)
    low_iota = lax.broadcasted_iota(jnp.int32, (LOW, CHAN_DEV), 0)
    for src in range(GROUPS):
        delay = tabs[src, 0:1, :]
        columns = slice(src * CHAN_DEV, (src + 1) * CHAN_DEV)
        onehot[:, columns] = jnp.where(low_iota == delay % LOW, 1.0, 0.0).astype(jnp.bfloat16)
        high = jnp.broadcast_to(delay // LOW % QUARTERS, (2 * BEAMS, CHAN_DEV))
        for q in range(QUARTERS):
            quarter[q * 16 : (q + 1) * 16, columns] = jnp.where(high == q, 1.0, 0.0).astype(
                jnp.bfloat16
            )
    lane = lax.broadcasted_iota(jnp.int32, (1, 128), 1)
    turns = []
    for g in range(8):
        step = tabs[4 * g + 3, 1:2, :]
        for q in range(3):
            step = jnp.where(
                lane // TRIAL_DEV == q, tabs[4 * g + q, 1:2, :], step
            )
        m = step * (me + 1) % SAMPLES
        turns.append(m)
        pick[:, g * 128 : (g + 1) * 128] = jnp.where(
            low_iota == m // QUARTERS, 1.0, 0.0
        ).astype(jnp.bfloat16)

    arrived(recv, spec_recv)
    for src in range(GROUPS):
        columns = slice(src * CHAN_DEV, (src + 1) * CHAN_DEV)
        spec = recv[src]
        for q in range(QUARTERS):
            masked[q * 16 : (q + 1) * 16, columns] = spec * quarter[q * 16 : (q + 1) * 16, columns]
    binned = dot_nt(masked[...], onehot[...])
    re = [binned[16 * q : 16 * q + 8] for q in range(4)]
    im = [binned[16 * q + 8 : 16 * q + 16] for q in range(4)]
    combined = [
        (re[0] + re[1] + re[2] + re[3], im[0] + im[1] + im[2] + im[3]),
        (re[0] - im[1] - re[2] + im[3], im[0] + re[1] - im[2] - re[3]),
        (re[0] - re[1] + re[2] - re[3], im[0] - im[1] + im[2] - im[3]),
        (re[0] + im[1] - re[2] - im[3], im[0] - re[1] - im[2] + re[3]),
    ]
    consts[1].wait()
    parts = []
    for q in range(QUARTERS):
        pair = jnp.concatenate(combined[q], axis=0)
        coarse = pair.astype(jnp.bfloat16)
        fine = (pair - coarse.astype(jnp.float32)).astype(jnp.bfloat16)
        turned = jnp.dot(
            jnp.concatenate([coarse, fine], axis=0), twiddle[q], preferred_element_type=jnp.float32
        )
        turned = turned[0:16] + turned[16:32]
        real = turned[0:8, :LOW] - turned[8:16, LOW:]
        imag = turned[0:8, LOW:] + turned[8:16, :LOW]
        both = jnp.concatenate([real, imag], axis=0) / math.sqrt(CHANNELS)
        parts.append(both.astype(jnp.bfloat16))
    picked = jnp.dot(jnp.concatenate(parts, axis=0), pick[...], preferred_element_type=jnp.float32)

    sub = lax.broadcasted_iota(jnp.int32, (8, 128), 0)
    lanes = lax.broadcasted_iota(jnp.int32, (8, 128), 1)
    left = lanes < 64
    even = lanes % 64 < 32
    top = sub < 4
    for g in range(8):
        m = turns[g] % QUARTERS
        halves = []
        for r in range(2):
            chosen = None
            for q in range(QUARTERS):
                value = picked[q * 16 + r * 8 : q * 16 + r * 8 + 8, g * 128 : (g + 1) * 128]
                chosen = value if chosen is None else jnp.where(m == q, value, chosen)
            halves.append(chosen)
        a, b = halves
        mixed = (
            jnp.where(left, a, pltpu.roll(b, 64, 1)),
            jnp.where(left, pltpu.roll(a, 64, 1), b),
        )
        for pair in range(2):
            v = mixed[pair]
            swap = jnp.where(even, pltpu.roll(v, 96, 1), pltpu.roll(v, 32, 1))
            swap = pltpu.roll(swap, 4, 0)
            v = jnp.where(top == even, v, swap).astype(jnp.bfloat16)
            ded[4 * g + 2 * pair] = v[0:4]
            ded[4 * g + 2 * pair + 1] = v[4:8]

    exchange(lambda peer: ded.at[peer], ded_in, ded_send, ded_recv)
    ded_in[me] = ded[me]
    arrived(tabs, tab_send)
    arrived(recv, spec_send)
    consts[2].wait()
    arrived(ded_in, ded_recv)
    for src in range(GROUPS):
        rows[4 * src : 4 * src + 4] = ded_in[src].astype(jnp.float32)
    moved = rows[...].T.astype(jnp.bfloat16)
    series = jnp.dot(moved[0:64], spread[0], preferred_element_type=jnp.float32)
    series += jnp.dot(moved[64:128], spread[1], preferred_element_type=jnp.float32)
    series = series / math.sqrt(BINS)
    for high in range(2):
        for p in range(4):
            out_ref[4 * high + p] = series[32 * high : 32 * high + 32, 128 * p : 128 * (p + 1)]
    arrived(ded_in, ded_send)


def per_device(samples, trial_steps, chan_delay):
    forward, twiddle, spread = tables()
    anywhere = pl.BlockSpec(memory_space=pl.ANY)
    vmem = pl.BlockSpec(memory_space=pltpu.VMEM)
    bf16, f32, i32 = jnp.bfloat16, jnp.float32, jnp.int32
    dma = pltpu.SemaphoreType.DMA
    return pl.pallas_call(
        kernel,
        out_shape=jax.ShapeDtypeStruct((BEAMS, TRIAL_DEV, OUT_SAMPLES), f32),
        in_specs=[anywhere, vmem, vmem, anywhere, anywhere, anywhere],
        out_specs=vmem,
        scratch_shapes=[
            pltpu.VMEM((BEAMS, CHAN_DEV, SAMPLES), bf16),
            pltpu.VMEM((2 * BINS, SAMPLES), bf16),
            pltpu.VMEM((QUARTERS, LOW, 2 * LOW), bf16),
            pltpu.VMEM((2, 4 * BINS, 4 * OUT_SAMPLES), bf16),
            pltpu.VMEM((2, CHAN_DEV), i32),
            pltpu.VMEM((GROUPS, 2, CHAN_DEV), i32),
            pltpu.VMEM((BINS * 2 * BEAMS, CHAN_DEV), f32),
            pltpu.VMEM((BINS, 2 * BEAMS, CHAN_DEV), bf16),
            pltpu.VMEM((GROUPS, 2 * BEAMS, CHAN_DEV), bf16),
            pltpu.VMEM((LOW, CHANNELS), bf16),
            pltpu.VMEM((QUARTERS * 2 * BEAMS, CHANNELS), bf16),
            pltpu.VMEM((QUARTERS * 2 * BEAMS, CHANNELS), bf16),
            pltpu.VMEM((LOW, TRIALS), bf16),
            pltpu.VMEM((GROUPS, 4, 128), bf16),
            pltpu.VMEM((GROUPS, 4, 128), bf16),
            pltpu.VMEM((GROUPS * 4, 128), f32),
            dma((4,)),
            dma((3,)),
            dma(()),
            dma(()),
            dma(()),
            dma(()),
            dma(()),
            dma(()),
        ],
        compiler_params=pltpu.CompilerParams(
            collective_id=0, has_side_effects=True, vmem_limit_bytes=40 << 20
        ),
    )(
        samples,
        trial_steps.reshape(1, TRIAL_DEV),
        chan_delay.reshape(1, CHAN_DEV),
        forward,
        twiddle,
        spread,
    )


def solution(mesh):
    in_specs = (P("beam", "chan", None), P("chan"), P("chan"))
    out_specs = P("beam", "chan", None)
    return jax.shard_map(
        per_device, mesh=mesh, in_specs=in_specs, out_specs=out_specs, check_vma=False
    )
```

```python
import math

import jax
import jax.numpy as jnp
import numpy as np
from jax import lax
from jax.experimental import pallas as pl
from jax.experimental.pallas import tpu as pltpu
from jax.sharding import PartitionSpec as P

CHANNELS = 4096
SAMPLES = 1024
BINS = 32
TRIALS = 1024
OUT_SAMPLES = 128
EPSILON = 1e-05

GROUPS = 32
BEAMS = 8
CHAN_DEV = CHANNELS // GROUPS
TRIAL_DEV = TRIALS // GROUPS
LOW = 256
QUARTERS = SAMPLES // LOW
SIDES = (2, 4, 4)


def hops(offset):
    return sum(min(d, n - d) for d, n in zip(offset, SIDES))


OFFSETS = sorted(
    [(x, y, z) for x in range(2) for y in range(4) for z in range(4) if (x, y, z) != (0, 0, 0)],
    key=lambda offset: -hops(offset),
)


def turn(phase, period):
    return (phase % period).astype(np.float32) * np.float32(2.0 * math.pi / period)


def tables():
    bins = np.arange(1, BINS + 1)
    angle = turn(bins[:, None] * np.arange(SAMPLES)[None, :], SAMPLES)
    forward = np.concatenate([np.cos(angle), -np.sin(angle)])
    low = np.arange(LOW)
    m = np.arange(QUARTERS)[:, None, None] + QUARTERS * low[None, None, :]
    angle = turn(m * low[None, :, None], SAMPLES)
    twiddle = np.concatenate([np.cos(angle), np.sin(angle)], 2)
    angle = turn(bins[:, None] * np.arange(OUT_SAMPLES)[None, :], OUT_SAMPLES)
    backward = np.stack([np.cos(angle), -np.sin(angle)])
    spread = np.zeros((2, BINS, 4, 4, OUT_SAMPLES), np.float32)
    for p in range(4):
        spread[:, :, p, p] = backward
    spread = spread.reshape(2, BINS * 4, 4 * OUT_SAMPLES)
    return [jnp.asarray(t, jnp.bfloat16) for t in (forward, twiddle, spread)]


def dot_nt(a, b):
    return lax.dot_general(a, b, (((1,), (1,)), ((), ())), preferred_element_type=jnp.float32)


def kernel(
    samples_ref, steps_hbm, delay_hbm, forward_hbm, twiddle_hbm, spread_hbm, out_ref,
    samp, steps_ref, delay_ref, forward, twiddle, spread, tab, tabs, plain, send, recv, onehot, quarter, masked, pick,
    ded, ded_in, rows, in_sem, const_sem, tab_send, tab_recv, spec_send, spec_recv, ded_send, ded_recv,
):
    me = lax.axis_index("chan")
    mx, my, mz = me // 16, (me // 4) % 4, me % 4
    xs = [(mx + d) % 2 for d in range(2)]
    ys = [(my + d) % 4 for d in range(4)]
    zs = [(mz + d) % 4 for d in range(4)]
    peers = [xs[x] * 16 + ys[y] * 4 + zs[z] for x, y, z in OFFSETS]

    loads = [
        pltpu.make_async_copy(
            samples_ref.at[pl.ds(2 * i, 2)], samp.at[pl.ds(2 * i, 2)], in_sem.at[i]
        )
        for i in range(4)
    ]
    consts = [
        pltpu.make_async_copy(src, dst, const_sem.at[i])
        for i, (src, dst) in enumerate(
            (
                (forward_hbm, forward),
                (twiddle_hbm, twiddle),
                (spread_hbm, spread),
                (steps_hbm, steps_ref),
                (delay_hbm, delay_ref),
            )
        )
    ]
    consts[0].start()
    for load in loads:
        load.start()
    consts[3].start()
    consts[4].start()
    consts[1].start()
    consts[2].start()

    barrier = pltpu.get_barrier_semaphore()
    for peer in peers:
        pl.semaphore_signal(
            barrier, inc=1, device_id={"chan": peer}, device_id_type=pl.DeviceIdType.MESH
        )

    consts[3].wait()
    consts[4].wait()
    steps = steps_ref[...]
    tab[0:1, :] = delay_ref[...]
    tab[1:2, :] = jnp.concatenate([steps] * (CHAN_DEV // TRIAL_DEV), axis=1)

    consts[0].wait()
    for i in range(4):
        loads[i].wait()
        block = samp[2 * i : 2 * i + 2].reshape(2 * CHAN_DEV, SAMPLES)
        product = dot_nt(forward[...], block)
        energy = jnp.zeros((2 * CHAN_DEV, 128), jnp.float32)
        for j in range(SAMPLES // 128):
            piece = block[:, 128 * j : 128 * (j + 1)].astype(jnp.float32)
            energy += piece * piece
        energy = jnp.sum(energy.T, axis=0, keepdims=True)
        scaling = 1.0 / jnp.sqrt(energy / SAMPLES + EPSILON) / math.sqrt(SAMPLES)
        product = product * scaling
        for half in range(2):
            for r in range(2):
                plain[pl.ds(r * BEAMS + 2 * i + half, BINS, stride=2 * BEAMS), :] = product[
                    r * BINS : (r + 1) * BINS, half * CHAN_DEV : (half + 1) * CHAN_DEV
                ]
    send[...] = plain[...].astype(jnp.bfloat16).reshape(BINS, 2 * BEAMS, CHAN_DEV)

    pl.semaphore_wait(barrier, GROUPS - 1)

    def exchange(pick_src, dst, send_sem, recv_sem):
        for n, peer in enumerate(peers):
            pltpu.make_async_remote_copy(
                src_ref=pick_src(peer),
                dst_ref=dst.at[me],
                send_sem=send_sem,
                recv_sem=recv_sem,
                device_id={"chan": peer},
                device_id_type=pl.DeviceIdType.MESH,
            ).start()

    def arrived(buffer, sem):
        part = buffer.at[pl.ds(0, GROUPS - 1)]
        pltpu.make_async_copy(part, part, sem).wait()

    exchange(lambda peer: tab, tabs, tab_send, tab_recv)
    exchange(lambda peer: send.at[peer], recv, spec_send, spec_recv)

    tabs[me] = tab[...]
    recv[me] = send[me]

    arrived(tabs, tab_recv)
    low_iota = lax.broadcasted_iota(jnp.int32, (LOW, CHAN_DEV), 0)
    for src in range(GROUPS):
        delay = tabs[src, 0:1, :]
        columns = slice(src * CHAN_DEV, (src + 1) * CHAN_DEV)
        onehot[:, columns] = jnp.where(low_iota == delay % LOW, 1.0, 0.0).astype(jnp.bfloat16)
        high = jnp.broadcast_to(delay // LOW % QUARTERS, (2 * BEAMS, CHAN_DEV))
        for q in range(QUARTERS):
            quarter[q * 16 : (q + 1) * 16, columns] = jnp.where(high == q, 1.0, 0.0).astype(
                jnp.bfloat16
            )
    lane = lax.broadcasted_iota(jnp.int32, (1, 128), 1)
    turns = []
    for g in range(8):
        step = tabs[4 * g + 3, 1:2, :]
        for q in range(3):
            step = jnp.where(
                lane // TRIAL_DEV == q, tabs[4 * g + q, 1:2, :], step
            )
        m = step * (me + 1) % SAMPLES
        turns.append(m)
        pick[:, g * 128 : (g + 1) * 128] = jnp.where(
            low_iota == m // QUARTERS, 1.0, 0.0
        ).astype(jnp.bfloat16)

    arrived(recv, spec_recv)
    for src in range(GROUPS):
        columns = slice(src * CHAN_DEV, (src + 1) * CHAN_DEV)
        spec = recv[src]
        for q in range(QUARTERS):
            masked[q * 16 : (q + 1) * 16, columns] = spec * quarter[q * 16 : (q + 1) * 16, columns]
    binned = dot_nt(masked[...], onehot[...])
    re = [binned[16 * q : 16 * q + 8] for q in range(4)]
    im = [binned[16 * q + 8 : 16 * q + 16] for q in range(4)]
    combined = [
        (re[0] + re[1] + re[2] + re[3], im[0] + im[1] + im[2] + im[3]),
        (re[0] - im[1] - re[2] + im[3], im[0] + re[1] - im[2] - re[3]),
        (re[0] - re[1] + re[2] - re[3], im[0] - im[1] + im[2] - im[3]),
        (re[0] + im[1] - re[2] - im[3], im[0] - re[1] - im[2] + re[3]),
    ]
    consts[1].wait()
    parts = []
    for q in range(QUARTERS):
        pair = jnp.concatenate(combined[q], axis=0)
        coarse = pair.astype(jnp.bfloat16)
        fine = (pair - coarse.astype(jnp.float32)).astype(jnp.bfloat16)
        turned = jnp.dot(
            jnp.concatenate([coarse, fine], axis=0), twiddle[q], preferred_element_type=jnp.float32
        )
        turned = turned[0:16] + turned[16:32]
        real = turned[0:8, :LOW] - turned[8:16, LOW:]
        imag = turned[0:8, LOW:] + turned[8:16, :LOW]
        both = jnp.concatenate([real, imag], axis=0) / math.sqrt(CHANNELS)
        parts.append(both.astype(jnp.bfloat16))
    picked = jnp.dot(jnp.concatenate(parts, axis=0), pick[...], preferred_element_type=jnp.float32)

    sub = lax.broadcasted_iota(jnp.int32, (8, 128), 0)
    lanes = lax.broadcasted_iota(jnp.int32, (8, 128), 1)
    left = lanes < 64
    even = lanes % 64 < 32
    top = sub < 4
    for g in range(8):
        m = turns[g] % QUARTERS
        halves = []
        for r in range(2):
            chosen = None
            for q in range(QUARTERS):
                value = picked[q * 16 + r * 8 : q * 16 + r * 8 + 8, g * 128 : (g + 1) * 128]
                chosen = value if chosen is None else jnp.where(m == q, value, chosen)
            halves.append(chosen)
        a, b = halves
        mixed = (
            jnp.where(left, a, pltpu.roll(b, 64, 1)),
            jnp.where(left, pltpu.roll(a, 64, 1), b),
        )
        for pair in range(2):
            v = mixed[pair]
            swap = jnp.where(even, pltpu.roll(v, 96, 1), pltpu.roll(v, 32, 1))
            swap = pltpu.roll(swap, 4, 0)
            v = jnp.where(top == even, v, swap).astype(jnp.bfloat16)
            ded[4 * g + 2 * pair] = v[0:4]
            ded[4 * g + 2 * pair + 1] = v[4:8]

    exchange(lambda peer: ded.at[peer], ded_in, ded_send, ded_recv)
    ded_in[me] = ded[me]
    arrived(tabs, tab_send)
    arrived(recv, spec_send)
    consts[2].wait()
    arrived(ded_in, ded_recv)
    for src in range(GROUPS):
        rows[4 * src : 4 * src + 4] = ded_in[src].astype(jnp.float32)
    moved = rows[...].T.astype(jnp.bfloat16)
    series = jnp.dot(moved[0:64], spread[0], preferred_element_type=jnp.float32)
    series += jnp.dot(moved[64:128], spread[1], preferred_element_type=jnp.float32)
    series = series / math.sqrt(BINS)
    for high in range(2):
        for p in range(4):
            out_ref[4 * high + p] = series[32 * high : 32 * high + 32, 128 * p : 128 * (p + 1)]
    arrived(ded_in, ded_send)


def per_device(samples, trial_steps, chan_delay):
    forward, twiddle, spread = tables()
    hbm = pl.BlockSpec(memory_space=pltpu.HBM)
    vmem = pl.BlockSpec(memory_space=pltpu.VMEM)
    bf16, f32, i32 = jnp.bfloat16, jnp.float32, jnp.int32
    dma = pltpu.SemaphoreType.DMA
    return pl.pallas_call(
        kernel,
        out_shape=pltpu.VMEM((BEAMS, TRIAL_DEV, OUT_SAMPLES), f32),
        in_specs=[hbm] * 6,
        out_specs=vmem,
        scratch_shapes=[
            pltpu.VMEM((BEAMS, CHAN_DEV, SAMPLES), bf16),
            pltpu.VMEM((1, TRIAL_DEV), i32),
            pltpu.VMEM((1, CHAN_DEV), i32),
            pltpu.VMEM((2 * BINS, SAMPLES), bf16),
            pltpu.VMEM((QUARTERS, LOW, 2 * LOW), bf16),
            pltpu.VMEM((2, 4 * BINS, 4 * OUT_SAMPLES), bf16),
            pltpu.VMEM((2, CHAN_DEV), i32),
            pltpu.VMEM((GROUPS, 2, CHAN_DEV), i32),
            pltpu.VMEM((BINS * 2 * BEAMS, CHAN_DEV), f32),
            pltpu.VMEM((BINS, 2 * BEAMS, CHAN_DEV), bf16),
            pltpu.VMEM((GROUPS, 2 * BEAMS, CHAN_DEV), bf16),
            pltpu.VMEM((LOW, CHANNELS), bf16),
            pltpu.VMEM((QUARTERS * 2 * BEAMS, CHANNELS), bf16),
            pltpu.VMEM((QUARTERS * 2 * BEAMS, CHANNELS), bf16),
            pltpu.VMEM((LOW, TRIALS), bf16),
            pltpu.VMEM((GROUPS, 4, 128), bf16),
            pltpu.VMEM((GROUPS, 4, 128), bf16),
            pltpu.VMEM((GROUPS * 4, 128), f32),
            dma((4,)),
            dma((5,)),
            dma(()),
            dma(()),
            dma(()),
            dma(()),
            dma(()),
            dma(()),
        ],
        compiler_params=pltpu.CompilerParams(
            collective_id=0, has_side_effects=True
        ),
    )(
        samples,
        trial_steps.reshape(1, TRIAL_DEV),
        chan_delay.reshape(1, CHAN_DEV),
        forward,
        twiddle,
        spread,
    )


def solution(mesh):
    in_specs = (P("beam", "chan", None), P("chan"), P("chan"))
    out_specs = P("beam", "chan", None)
    return jax.shard_map(
        per_device, mesh=mesh, in_specs=in_specs, out_specs=out_specs, check_vma=False
    )
```

```python
import math

import jax
import jax.numpy as jnp
import numpy as np
from jax import lax
from jax.experimental import pallas as pl
from jax.experimental.pallas import tpu as pltpu
from jax.sharding import PartitionSpec as P

CHANNELS = 4096
SAMPLES = 1024
BINS = 32
TRIALS = 1024
OUT_SAMPLES = 128
EPSILON = 1e-05

GROUPS = 32
BEAMS = 8
CHAN_DEV = CHANNELS // GROUPS
TRIAL_DEV = TRIALS // GROUPS
LOW = 256
QUARTERS = SAMPLES // LOW
MESH = pl.DeviceIdType.MESH


def chan_of(x, y, z):
    return x * 16 + y * 4 + z


PLANES = 2
OWNERS = 8 * PLANES
OWNED = BINS // OWNERS
TURNS = ((1, 2), (0, 2), (1, 1), (1, 3), (0, 1), (0, 3), (1, 0), (0, 0))
TO_OWNERS = [(x, y, z) for x, y in TURNS for z in range(PLANES)]
TO_ALL = [(x, y, z) for z in range(4) for x, y in TURNS]
PAIRS = [
    (y, z)
    for z, y in (
        (0, 0), (0, 1), (0, 3), (0, 2), (1, 0), (2, 0), (1, 1), (3, 0),
        (1, 3), (1, 2), (2, 1), (2, 3), (2, 2), (3, 1), (3, 3), (3, 2),
    )
]
LATE = 3
ROWS = 2 * BEAMS


def turn(phase, period):
    return (phase % period).astype(np.float32) * np.float32(2.0 * math.pi / period)


def tables():
    bins = np.arange(1, BINS + 1)
    angle = turn(bins[:, None] * np.arange(SAMPLES)[None, :], SAMPLES)
    forward = np.concatenate([np.cos(angle), -np.sin(angle)])
    low = np.arange(LOW)
    m = np.arange(QUARTERS)[:, None, None] + QUARTERS * low[None, None, :]
    angle = turn(m * low[None, :, None], SAMPLES)
    twiddle = np.concatenate([np.cos(angle), np.sin(angle)], 2)
    angle = turn(bins[:, None] * np.arange(OUT_SAMPLES)[None, :], OUT_SAMPLES)
    backward = np.stack([np.cos(angle), -np.sin(angle)])
    spread = np.zeros((2, BINS, 4, 4, OUT_SAMPLES), np.float32)
    for p in range(4):
        spread[:, :, p, p] = backward
    spread = spread.reshape(2, BINS * 4, 4 * OUT_SAMPLES)
    return [jnp.asarray(t, jnp.bfloat16) for t in (forward, twiddle, spread)]


def dot_nt(a, b):
    return lax.dot_general(a, b, (((1,), (1,)), ((), ())), preferred_element_type=jnp.float32)


def dot(a, b):
    return jnp.dot(a, b, preferred_element_type=jnp.float32)


def kernel(
    samples_hbm, steps_hbm, delay_hbm, forward_hbm, twiddle_hbm, spread_hbm, out_ref,
    samp, steps, delay, forward, twiddle, spread, tab, tabs, plain, send, recv, pick,
    ded, ded_in, rows, in_sem, const_sem, tab_send, tab_recv, spec_send, spec_recv, ded_send, ded_recv,
):
    me = lax.axis_index("chan")
    mx, my, mz = me // 16, me // 4 % 4, me % 4
    owner = jnp.where(mz < PLANES, 1, 0)
    rank = (me // 4) * PLANES + mz
    columns = {(x, y): (mx + x) % 2 * 16 + (my + y) % 4 * 4 for x, y in TURNS}

    small = [
        pltpu.make_async_copy(src, dst, const_sem.at[i])
        for i, (src, dst) in enumerate(
            (
                (steps_hbm, steps),
                (delay_hbm, delay),
                (forward_hbm, forward),
                (twiddle_hbm, twiddle),
                (spread_hbm, spread),
            )
        )
    ]
    loads = [
        pltpu.make_async_copy(samples_hbm.at[i], samp.at[i], in_sem.at[i]) for i in range(BEAMS)
    ]
    for copy in small[:3] + loads + small[3:]:
        copy.start()

    barrier = pltpu.get_barrier_semaphore()

    @pl.when(owner == 1)
    def _():
        for peer in [columns[x, y] + z for x, y in TURNS for z in (3, 2, 1, 0)]:

            @pl.when(peer != me)
            def _():
                pl.semaphore_signal(barrier, inc=1, device_id={"chan": peer}, device_id_type=MESH)

    small[0].wait()
    small[1].wait()
    tab[0:1, :] = delay[...]
    tab[1:2, :] = jnp.concatenate([steps[...]] * (CHAN_DEV // TRIAL_DEV), axis=1)
    small[2].wait()

    def spectrum(i):
        loads[2 * i].wait()
        loads[2 * i + 1].wait()
        block = samp[2 * i : 2 * i + 2].reshape(2 * CHAN_DEV, SAMPLES)
        product = dot_nt(forward[...], block)
        energy = jnp.zeros((2 * CHAN_DEV, 128), jnp.float32)
        for j in range(SAMPLES // 128):
            piece = block[:, 128 * j : 128 * (j + 1)].astype(jnp.float32)
            energy += piece * piece
        energy = jnp.sum(energy.T, axis=0, keepdims=True)
        scaling = 1.0 / jnp.sqrt(energy / SAMPLES + EPSILON) / math.sqrt(SAMPLES)
        product = product * scaling
        for half in range(2):
            for r in range(2):
                plain[pl.ds(r * BEAMS + 2 * i + half, BINS, stride=ROWS), :] = product[
                    r * BINS : (r + 1) * BINS, half * CHAN_DEV : (half + 1) * CHAN_DEV
                ]

    def post(src, dst, send_sem, recv_sem, peer):
        @pl.when(peer != me)
        def _():
            pltpu.make_async_remote_copy(
                src_ref=src,
                dst_ref=dst,
                send_sem=send_sem,
                recv_sem=recv_sem,
                device_id={"chan": peer},
                device_id_type=MESH,
            ).start()

    def keep(src, dst, sem):
        pltpu.make_async_copy(src, dst, sem).start()

    def arrived(part, sem):
        pltpu.make_async_copy(part, part, sem).wait()

    slot = me % 16
    for i in range(3):
        spectrum(i)
    pl.semaphore_wait(barrier, OWNERS - owner)
    for x, y, z in TO_OWNERS:
        peer = columns[x, y] + z
        post(tab, tabs.at[me], tab_send, tab_recv.at[slot], peer)

    @pl.when(owner == 1)
    def _():
        keep(tab, tabs.at[me], tab_recv.at[slot])

    spectrum(3)
    send[...] = plain[...].astype(jnp.bfloat16).reshape(BINS, ROWS, CHAN_DEV)
    for x, y, z in TO_OWNERS:
        peer = columns[x, y] + z
        first = (columns[x, y] // 4 * PLANES + z) * OWNED
        post(send.at[pl.ds(first, OWNED)], recv.at[me], spec_send, spec_recv.at[slot], peer)

    def dedisperse():
        low_iota = lax.broadcasted_iota(jnp.int32, (LOW, CHAN_DEV), 0)

        def binning(y, z):
            arrived(recv.at[pl.ds(0, 2)], spec_recv.at[4 * y + z])
            left, right = [], []
            for x in range(2):
                src = chan_of(x, y, z)
                place = tabs[src, 0:1, :]
                right.append(
                    jnp.where(low_iota == place % LOW, 1.0, 0.0).astype(jnp.bfloat16)
                )
                high = jnp.broadcast_to(place // LOW % QUARTERS, (ROWS, CHAN_DEV))
                masks = [
                    jnp.where(high == q, 1.0, 0.0).astype(jnp.bfloat16) for q in range(QUARTERS)
                ]
                left.append(
                    jnp.concatenate(
                        [recv[src, k] * masks[q] for k in range(OWNED) for q in range(QUARTERS)],
                        axis=0,
                    )
                )
            return dot_nt(jnp.concatenate(left, axis=1), jnp.concatenate(right, axis=1))

        def placed(y, z):
            arrived(tabs.at[pl.ds(0, 2)], tab_recv.at[4 * y + z])

        binned = None
        for y, z in PAIRS[:-LATE]:
            placed(y, z)
            part = binning(y, z)
            binned = part if binned is None else binned + part
        for y, z in PAIRS[-LATE:]:
            placed(y, z)
        lane = lax.broadcasted_iota(jnp.int32, (1, 128), 1)
        turns = [[] for _ in range(OWNED)]
        for g in range(8):
            step = tabs[4 * g + 3, 1:2, :]
            for q in range(3):
                step = jnp.where(lane // TRIAL_DEV == q, tabs[4 * g + q, 1:2, :], step)
            for k in range(OWNED):
                m = step * (rank * OWNED + k + 1) % SAMPLES
                turns[k].append(m % QUARTERS)
                pick[k, :, g * 128 : (g + 1) * 128] = jnp.where(
                    low_iota == m // QUARTERS, 1.0, 0.0
                ).astype(jnp.bfloat16)
        small[3].wait()
        for y, z in PAIRS[-LATE:]:
            binned = binned + binning(y, z)

        parts = []
        for q in range(QUARTERS):
            stack = []
            for k in range(OWNED):
                base = k * QUARTERS * ROWS
                re = [binned[base + ROWS * j : base + ROWS * j + 8] for j in range(QUARTERS)]
                im = [binned[base + ROWS * j + 8 : base + ROWS * j + 16] for j in range(QUARTERS)]
                if q == 0:
                    pair = (re[0] + re[1] + re[2] + re[3], im[0] + im[1] + im[2] + im[3])
                elif q == 1:
                    pair = (re[0] - im[1] - re[2] + im[3], im[0] + re[1] - im[2] - re[3])
                elif q == 2:
                    pair = (re[0] - re[1] + re[2] - re[3], im[0] - im[1] + im[2] - im[3])
                else:
                    pair = (re[0] + im[1] - re[2] - im[3], im[0] - re[1] - im[2] + re[3])
                pair = jnp.concatenate(pair, axis=0)
                coarse = pair.astype(jnp.bfloat16)
                stack += [coarse, (pair - coarse.astype(jnp.float32)).astype(jnp.bfloat16)]
            turned = dot(jnp.concatenate(stack, axis=0), twiddle[q])
            parts.append([])
            for k in range(OWNED):
                both = turned[32 * k : 32 * k + 16] + turned[32 * k + 16 : 32 * k + 32]
                real = both[0:8, :LOW] - both[8:16, LOW:]
                imag = both[0:8, LOW:] + both[8:16, :LOW]
                both = jnp.concatenate([real, imag], axis=0) / math.sqrt(CHANNELS)
                parts[q].append(both.astype(jnp.bfloat16))

        sub = lax.broadcasted_iota(jnp.int32, (8, 128), 0)
        lanes = lax.broadcasted_iota(jnp.int32, (8, 128), 1)
        left = lanes < 64
        even = lanes % 64 < 32
        stay = (sub < 4) == even
        for k in range(OWNED):
            table = jnp.concatenate([parts[q][k] for q in range(QUARTERS)], axis=0)
            picked = dot(table, pick[k])
            for g in range(8):
                halves = []
                for r in range(2):
                    chosen = None
                    for q in range(QUARTERS):
                        at = q * ROWS + r * 8
                        value = picked[at : at + 8, g * 128 : (g + 1) * 128]
                        chosen = value if q == 0 else jnp.where(turns[k][g] == q, value, chosen)
                    halves.append(chosen)
                a, b = halves
                mixed = (
                    jnp.where(left, a, pltpu.roll(b, 64, 1)),
                    jnp.where(left, pltpu.roll(a, 64, 1), b),
                )
                for pair in range(2):
                    v = mixed[pair]
                    swap = jnp.where(even, pltpu.roll(v, 96, 1), pltpu.roll(v, 32, 1))
                    v = jnp.where(stay, v, pltpu.roll(swap, 4, 0)).astype(jnp.bfloat16)
                    ded[4 * g + 2 * pair, k] = v[0:4]
                    ded[4 * g + 2 * pair + 1, k] = v[4:8]

    own = pl.ds(rank * OWNED, OWNED)

    @pl.when(owner == 1)
    def _():
        keep(send.at[own], recv.at[me], spec_recv.at[slot])
        dedisperse()
        for x, y, z in TO_ALL:
            peer = columns[x, y] + z
            post(ded.at[peer], ded_in.at[own], ded_send, ded_recv, peer)
        keep(ded.at[me], ded_in.at[own], ded_recv)
        arrived(tabs.at[pl.ds(0, OWNERS - 1)], tab_send)
        arrived(recv.at[pl.ds(0, OWNERS - 1)], spec_send)

    @pl.when(owner == 0)
    def _():
        small[3].wait()
        arrived(tabs.at[pl.ds(0, OWNERS)], tab_send)
        arrived(recv.at[pl.ds(0, OWNERS)], spec_send)

    small[4].wait()
    arrived(ded_in, ded_recv)
    for src in range(GROUPS):
        rows[4 * src : 4 * src + 4] = ded_in[src].astype(jnp.float32)
    moved = rows[...].T.astype(jnp.bfloat16)
    series = dot(moved[0:64], spread[0]) + dot(moved[64:128], spread[1])
    series = series / math.sqrt(BINS)
    for high in range(2):
        for p in range(4):
            out_ref[4 * high + p] = series[32 * high : 32 * high + 32, 128 * p : 128 * (p + 1)]

    @pl.when(owner == 1)
    def _():
        arrived(ded.at[pl.ds(0, GROUPS - 1)], ded_send)


def per_device(samples, trial_steps, chan_delay):
    forward, twiddle, spread = tables()
    hbm = pl.BlockSpec(memory_space=pltpu.HBM)
    bf16, f32, i32 = jnp.bfloat16, jnp.float32, jnp.int32
    dma = pltpu.SemaphoreType.DMA
    return pl.pallas_call(
        kernel,
        out_shape=pltpu.VMEM((BEAMS, TRIAL_DEV, OUT_SAMPLES), f32),
        in_specs=[hbm] * 6,
        out_specs=pl.BlockSpec(memory_space=pltpu.VMEM),
        scratch_shapes=[
            pltpu.VMEM((BEAMS, CHAN_DEV, SAMPLES), bf16),
            pltpu.VMEM((1, TRIAL_DEV), i32),
            pltpu.VMEM((1, CHAN_DEV), i32),
            pltpu.VMEM((2 * BINS, SAMPLES), bf16),
            pltpu.VMEM((QUARTERS, LOW, 2 * LOW), bf16),
            pltpu.VMEM((2, 4 * BINS, 4 * OUT_SAMPLES), bf16),
            pltpu.VMEM((2, CHAN_DEV), i32),
            pltpu.VMEM((GROUPS, 2, CHAN_DEV), i32),
            pltpu.VMEM((BINS * ROWS, CHAN_DEV), f32),
            pltpu.VMEM((BINS, ROWS, CHAN_DEV), bf16),
            pltpu.VMEM((GROUPS, OWNED, ROWS, CHAN_DEV), bf16),
            pltpu.VMEM((OWNED, LOW, TRIALS), bf16),
            pltpu.VMEM((GROUPS, OWNED, 4, 128), bf16),
            pltpu.VMEM((BINS, 4, 128), bf16),
            pltpu.VMEM((GROUPS * 4, 128), f32),
            dma((BEAMS,)),
            dma((5,)),
            dma(()),
            dma((len(PAIRS),)),
            dma(()),
            dma((len(PAIRS),)),
            dma(()),
            dma(()),
        ],
        compiler_params=pltpu.CompilerParams(collective_id=0, has_side_effects=True),
    )(
        samples,
        trial_steps.reshape(1, TRIAL_DEV),
        chan_delay.reshape(1, CHAN_DEV),
        forward,
        twiddle,
        spread,
    )


def solution(mesh):
    in_specs = (P("beam", "chan", None), P("chan"), P("chan"))
    out_specs = P("beam", "chan", None)
    return jax.shard_map(
        per_device, mesh=mesh, in_specs=in_specs, out_specs=out_specs, check_vma=False
    )
```

```python
import math

import jax
import jax.numpy as jnp
import numpy as np
from jax import lax
from jax.experimental import pallas as pl
from jax.experimental.pallas import tpu as pltpu
from jax.sharding import PartitionSpec as P

CHANNELS = 4096
SAMPLES = 1024
BINS = 32
TRIALS = 1024
OUT_SAMPLES = 128
EPSILON = 1e-05

GROUPS = 32
BEAMS = 8
CHAN_DEV = CHANNELS // GROUPS
TRIAL_DEV = TRIALS // GROUPS
LOW = 256
QUARTERS = SAMPLES // LOW
MESH = pl.DeviceIdType.MESH


def chan_of(x, y, z):
    return x * 16 + y * 4 + z


PLANES = 2
OWNERS = 8 * PLANES
OWNED = BINS // OWNERS
TURNS = ((1, 2), (0, 2), (1, 1), (1, 3), (0, 1), (0, 3), (1, 0), (0, 0))
TO_OWNERS = [(x, y, z) for x, y in TURNS for z in range(PLANES)]
TO_ALL = [(x, y, z) for z in range(4) for x, y in TURNS]
PAIRS = [
    (y, z)
    for z, y in (
        (0, 0), (0, 1), (0, 3), (0, 2), (1, 0), (2, 0), (1, 1), (3, 0),
        (1, 3), (1, 2), (2, 1), (2, 3), (2, 2), (3, 1), (3, 3), (3, 2),
    )
]
ROWS = 2 * BEAMS


def turn(phase, period):
    return (phase % period).astype(np.float32) * np.float32(2.0 * math.pi / period)


def tables():
    bins = np.arange(1, BINS + 1)
    angle = turn(bins[:, None] * np.arange(SAMPLES)[None, :], SAMPLES)
    forward = np.concatenate([np.cos(angle), -np.sin(angle)])
    low = np.arange(LOW)
    m = np.arange(QUARTERS)[:, None, None] + QUARTERS * low[None, None, :]
    angle = turn(m * low[None, :, None], SAMPLES)
    twiddle = np.concatenate([np.cos(angle), np.sin(angle)], 2)
    angle = turn(bins[:, None] * np.arange(OUT_SAMPLES)[None, :], OUT_SAMPLES)
    backward = np.stack([np.cos(angle), -np.sin(angle)])
    spread = np.zeros((2, BINS, 4, 4, OUT_SAMPLES), np.float32)
    for p in range(4):
        spread[:, :, p, p] = backward
    spread = spread.reshape(2, BINS * 4, 4 * OUT_SAMPLES)
    return [jnp.asarray(t, jnp.bfloat16) for t in (forward, twiddle, spread)]


def dot_nt(a, b):
    return lax.dot_general(a, b, (((1,), (1,)), ((), ())), preferred_element_type=jnp.float32)


def dot(a, b):
    return jnp.dot(a, b, preferred_element_type=jnp.float32)


def kernel(
    samples_hbm, steps_hbm, delay_hbm, forward_hbm, twiddle_hbm, spread_hbm, out_ref,
    samp, steps, delay, forward, twiddle, spread, tab, tabs, plain, send, recv, pick,
    ded, ded_in, rows, in_sem, const_sem, tab_send, tab_recv, spec_send, spec_recv, ded_send, ded_recv,
):
    me = lax.axis_index("chan")
    mx, my, mz = me // 16, me // 4 % 4, me % 4
    owner = jnp.where(mz < PLANES, 1, 0)
    rank = (me // 4) * PLANES + mz
    columns = {(x, y): (mx + x) % 2 * 16 + (my + y) % 4 * 4 for x, y in TURNS}

    small = [
        pltpu.make_async_copy(src, dst, const_sem.at[i])
        for i, (src, dst) in enumerate(
            (
                (steps_hbm, steps),
                (delay_hbm, delay),
                (forward_hbm, forward),
                (twiddle_hbm, twiddle),
                (spread_hbm, spread),
            )
        )
    ]
    loads = [
        pltpu.make_async_copy(samples_hbm.at[i], samp.at[i], in_sem.at[i]) for i in range(BEAMS)
    ]
    for copy in small[:3] + loads + small[3:]:
        copy.start()

    barrier = pltpu.get_barrier_semaphore()

    @pl.when(owner == 1)
    def _():
        for peer in [columns[x, y] + z for x, y in TURNS for z in (3, 2, 1, 0)]:

            @pl.when(peer != me)
            def _():
                pl.semaphore_signal(barrier, inc=1, device_id={"chan": peer}, device_id_type=MESH)

    small[0].wait()
    small[1].wait()
    tab[0:1, :] = delay[...]
    tab[1:2, :] = jnp.concatenate([steps[...]] * (CHAN_DEV // TRIAL_DEV), axis=1)
    small[2].wait()

    def spectrum(i):
        loads[2 * i].wait()
        loads[2 * i + 1].wait()
        block = samp[2 * i : 2 * i + 2].reshape(2 * CHAN_DEV, SAMPLES)
        product = dot_nt(forward[...], block)
        energy = jnp.zeros((2 * CHAN_DEV, 128), jnp.float32)
        for j in range(SAMPLES // 128):
            piece = block[:, 128 * j : 128 * (j + 1)].astype(jnp.float32)
            energy += piece * piece
        energy = jnp.sum(energy.T, axis=0, keepdims=True)
        scaling = 1.0 / jnp.sqrt(energy / SAMPLES + EPSILON) / math.sqrt(SAMPLES)
        product = product * scaling
        for half in range(2):
            for r in range(2):
                plain[pl.ds(r * BEAMS + 2 * i + half, BINS, stride=ROWS), :] = product[
                    r * BINS : (r + 1) * BINS, half * CHAN_DEV : (half + 1) * CHAN_DEV
                ]

    def post(src, dst, send_sem, recv_sem, peer):
        @pl.when(peer != me)
        def _():
            pltpu.make_async_remote_copy(
                src_ref=src,
                dst_ref=dst,
                send_sem=send_sem,
                recv_sem=recv_sem,
                device_id={"chan": peer},
                device_id_type=MESH,
            ).start()

    def keep(src, dst, sem):
        pltpu.make_async_copy(src, dst, sem).start()

    def arrived(part, sem):
        pltpu.make_async_copy(part, part, sem).wait()

    slot = me % 16
    for i in range(3):
        spectrum(i)
    pl.semaphore_wait(barrier, OWNERS - owner)
    for x, y, z in TO_OWNERS:
        peer = columns[x, y] + z
        post(tab, tabs.at[me], tab_send, tab_recv.at[slot], peer)

    @pl.when(owner == 1)
    def _():
        keep(tab, tabs.at[me], tab_recv.at[slot])

    spectrum(3)
    send[...] = plain[...].astype(jnp.bfloat16).reshape(BINS, ROWS, CHAN_DEV)
    for x, y, z in TO_OWNERS:
        peer = columns[x, y] + z
        first = (columns[x, y] // 4 * PLANES + z) * OWNED
        post(send.at[pl.ds(first, OWNED)], recv.at[me], spec_send, spec_recv.at[slot], peer)

    def dedisperse():
        low_iota = lax.broadcasted_iota(jnp.int32, (LOW, CHAN_DEV), 0).astype(jnp.float32).astype(jnp.bfloat16)
        one = jnp.ones((), jnp.bfloat16)
        zero = jnp.zeros((), jnp.bfloat16)

        def hot(index):
            row = jnp.broadcast_to(index.astype(jnp.float32), (16, CHAN_DEV)).astype(jnp.bfloat16)
            return jnp.where(low_iota == jnp.concatenate([row] * (LOW // 16), axis=0), one, zero)

        def binning(pairs):
            left, right = [], []
            for y, z in pairs:
                arrived(recv.at[pl.ds(0, 2)], spec_recv.at[4 * y + z])
            for y, z in pairs:
                for x in range(2):
                    src = chan_of(x, y, z)
                    place = tabs[src, 0:1, :]
                    right.append(hot(place % LOW))
                    high = jnp.broadcast_to(place // LOW % QUARTERS, (ROWS, CHAN_DEV))
                    masks = [
                        jnp.where(high == q, 1.0, 0.0).astype(jnp.bfloat16) for q in range(QUARTERS)
                    ]
                    left.append(
                        jnp.concatenate(
                            [recv[src, k] * masks[q] for k in range(OWNED) for q in range(QUARTERS)],
                            axis=0,
                        )
                    )
            return dot_nt(jnp.concatenate(left, axis=1), jnp.concatenate(right, axis=1))

        def placed(y, z):
            arrived(tabs.at[pl.ds(0, 2)], tab_recv.at[4 * y + z])

        for y, z in PAIRS:
            placed(y, z)
        lane = lax.broadcasted_iota(jnp.int32, (1, 128), 1)
        turns = [[] for _ in range(OWNED)]
        for g in range(8):
            step = tabs[4 * g + 3, 1:2, :]
            for q in range(3):
                step = jnp.where(lane // TRIAL_DEV == q, tabs[4 * g + q, 1:2, :], step)
            for k in range(OWNED):
                m = step * (rank * OWNED + k + 1) % SAMPLES
                turns[k].append(m % QUARTERS)
                pick[k, :, g * 128 : (g + 1) * 128] = hot(m // QUARTERS)
        small[3].wait()
        binned = binning(PAIRS)

        parts = []
        for q in range(QUARTERS):
            stack = []
            for k in range(OWNED):
                base = k * QUARTERS * ROWS
                re = [binned[base + ROWS * j : base + ROWS * j + 8] for j in range(QUARTERS)]
                im = [binned[base + ROWS * j + 8 : base + ROWS * j + 16] for j in range(QUARTERS)]
                if q == 0:
                    pair = (re[0] + re[1] + re[2] + re[3], im[0] + im[1] + im[2] + im[3])
                elif q == 1:
                    pair = (re[0] - im[1] - re[2] + im[3], im[0] + re[1] - im[2] - re[3])
                elif q == 2:
                    pair = (re[0] - re[1] + re[2] - re[3], im[0] - im[1] + im[2] - im[3])
                else:
                    pair = (re[0] + im[1] - re[2] - im[3], im[0] - re[1] - im[2] + re[3])
                pair = jnp.concatenate(pair, axis=0)
                coarse = pair.astype(jnp.bfloat16)
                stack += [coarse, (pair - coarse.astype(jnp.float32)).astype(jnp.bfloat16)]
            turned = dot(jnp.concatenate(stack, axis=0), twiddle[q])
            parts.append([])
            for k in range(OWNED):
                both = turned[32 * k : 32 * k + 16] + turned[32 * k + 16 : 32 * k + 32]
                real = both[0:8, :LOW] - both[8:16, LOW:]
                imag = both[0:8, LOW:] + both[8:16, :LOW]
                both = jnp.concatenate([real, imag], axis=0) / math.sqrt(CHANNELS)
                parts[q].append(both.astype(jnp.bfloat16))

        sub = lax.broadcasted_iota(jnp.int32, (8, 128), 0)
        lanes = lax.broadcasted_iota(jnp.int32, (8, 128), 1)
        left = lanes < 64
        even = lanes % 64 < 32
        stay = (sub < 4) == even
        for k in range(OWNED):
            table = jnp.concatenate([parts[q][k] for q in range(QUARTERS)], axis=0)
            picked = dot(table, pick[k])
            for g in range(8):
                halves = []
                for r in range(2):
                    chosen = None
                    for q in range(QUARTERS):
                        at = q * ROWS + r * 8
                        value = picked[at : at + 8, g * 128 : (g + 1) * 128]
                        chosen = value if q == 0 else jnp.where(turns[k][g] == q, value, chosen)
                    halves.append(chosen)
                a, b = halves
                mixed = (
                    jnp.where(left, a, pltpu.roll(b, 64, 1)),
                    jnp.where(left, pltpu.roll(a, 64, 1), b),
                )
                for pair in range(2):
                    v = mixed[pair]
                    swap = jnp.where(even, pltpu.roll(v, 96, 1), pltpu.roll(v, 32, 1))
                    v = jnp.where(stay, v, pltpu.roll(swap, 4, 0)).astype(jnp.bfloat16)
                    ded[4 * g + 2 * pair, k] = v[0:4]
                    ded[4 * g + 2 * pair + 1, k] = v[4:8]

    own = pl.ds(rank * OWNED, OWNED)

    @pl.when(owner == 1)
    def _():
        keep(send.at[own], recv.at[me], spec_recv.at[slot])
        dedisperse()
        for x, y, z in TO_ALL:
            peer = columns[x, y] + z
            post(ded.at[peer], ded_in.at[own], ded_send, ded_recv, peer)
        keep(ded.at[me], ded_in.at[own], ded_recv)
        arrived(tabs.at[pl.ds(0, OWNERS - 1)], tab_send)
        arrived(recv.at[pl.ds(0, OWNERS - 1)], spec_send)

    @pl.when(owner == 0)
    def _():
        small[3].wait()
        arrived(tabs.at[pl.ds(0, OWNERS)], tab_send)
        arrived(recv.at[pl.ds(0, OWNERS)], spec_send)

    small[4].wait()
    arrived(ded_in, ded_recv)
    for src in range(GROUPS):
        rows[4 * src : 4 * src + 4] = ded_in[src].astype(jnp.float32)
    moved = rows[...].T.astype(jnp.bfloat16)
    series = dot(moved[0:64], spread[0]) + dot(moved[64:128], spread[1])
    series = series / math.sqrt(BINS)
    for high in range(2):
        for p in range(4):
            out_ref[4 * high + p] = series[32 * high : 32 * high + 32, 128 * p : 128 * (p + 1)]

    @pl.when(owner == 1)
    def _():
        arrived(ded.at[pl.ds(0, GROUPS - 1)], ded_send)


def per_device(samples, trial_steps, chan_delay):
    forward, twiddle, spread = tables()
    hbm = pl.BlockSpec(memory_space=pltpu.HBM)
    bf16, f32, i32 = jnp.bfloat16, jnp.float32, jnp.int32
    dma = pltpu.SemaphoreType.DMA
    return pl.pallas_call(
        kernel,
        out_shape=pltpu.VMEM((BEAMS, TRIAL_DEV, OUT_SAMPLES), f32),
        in_specs=[hbm] * 6,
        out_specs=pl.BlockSpec(memory_space=pltpu.VMEM),
        scratch_shapes=[
            pltpu.VMEM((BEAMS, CHAN_DEV, SAMPLES), bf16),
            pltpu.VMEM((1, TRIAL_DEV), i32),
            pltpu.VMEM((1, CHAN_DEV), i32),
            pltpu.VMEM((2 * BINS, SAMPLES), bf16),
            pltpu.VMEM((QUARTERS, LOW, 2 * LOW), bf16),
            pltpu.VMEM((2, 4 * BINS, 4 * OUT_SAMPLES), bf16),
            pltpu.VMEM((2, CHAN_DEV), i32),
            pltpu.VMEM((GROUPS, 2, CHAN_DEV), i32),
            pltpu.VMEM((BINS * ROWS, CHAN_DEV), f32),
            pltpu.VMEM((BINS, ROWS, CHAN_DEV), bf16),
            pltpu.VMEM((GROUPS, OWNED, ROWS, CHAN_DEV), bf16),
            pltpu.VMEM((OWNED, LOW, TRIALS), bf16),
            pltpu.VMEM((GROUPS, OWNED, 4, 128), bf16),
            pltpu.VMEM((BINS, 4, 128), bf16),
            pltpu.VMEM((GROUPS * 4, 128), f32),
            dma((BEAMS,)),
            dma((5,)),
            dma(()),
            dma((len(PAIRS),)),
            dma(()),
            dma((len(PAIRS),)),
            dma(()),
            dma(()),
        ],
        compiler_params=pltpu.CompilerParams(collective_id=0, has_side_effects=True),
    )(
        samples,
        trial_steps.reshape(1, TRIAL_DEV),
        chan_delay.reshape(1, CHAN_DEV),
        forward,
        twiddle,
        spread,
    )


def solution(mesh):
    in_specs = (P("beam", "chan", None), P("chan"), P("chan"))
    out_specs = P("beam", "chan", None)
    return jax.shard_map(
        per_device, mesh=mesh, in_specs=in_specs, out_specs=out_specs, check_vma=False
    )
```

```python
import math

import jax
import jax.numpy as jnp
import numpy as np
from jax import lax
from jax.experimental import pallas as pl
from jax.experimental.pallas import tpu as pltpu
from jax.sharding import PartitionSpec as P

CHANNELS = 4096
SAMPLES = 1024
BINS = 32
TRIALS = 1024
OUT_SAMPLES = 128
EPSILON = 1e-05

GROUPS = 32
BEAMS = 8
CHAN_DEV = CHANNELS // GROUPS
TRIAL_DEV = TRIALS // GROUPS
LOW = 256
QUARTERS = SAMPLES // LOW
MESH = pl.DeviceIdType.MESH


def chan_of(x, y, z):
    return x * 16 + y * 4 + z


PLANES = 2
OWNERS = 8 * PLANES
OWNED = BINS // OWNERS
TURNS = ((1, 2), (0, 2), (1, 1), (1, 3), (0, 1), (0, 3), (1, 0), (0, 0))
TO_OWNERS = [(x, y, z) for x, y in TURNS for z in range(PLANES)]
TO_ALL = [(x, y, z) for z in range(4) for x, y in TURNS]
PAIRS = [
    (y, z)
    for z, y in (
        (0, 0), (0, 1), (0, 3), (0, 2), (1, 0), (2, 0), (1, 1), (3, 0),
        (1, 3), (1, 2), (2, 1), (2, 3), (2, 2), (3, 1), (3, 3), (3, 2),
    )
]
ROWS = 2 * BEAMS


def turn(phase, period):
    return (phase % period).astype(np.float32) * np.float32(2.0 * math.pi / period)


def tables():
    bins = np.arange(1, BINS + 1)
    angle = turn(bins[:, None] * np.arange(SAMPLES)[None, :], SAMPLES)
    forward = np.concatenate([np.cos(angle), -np.sin(angle)])
    low = np.arange(LOW)
    m = np.arange(QUARTERS)[:, None, None] + QUARTERS * low[None, None, :]
    angle = turn(m * low[None, :, None], SAMPLES)
    twiddle = np.concatenate([np.cos(angle), np.sin(angle)], 2)
    angle = turn(bins[:, None] * np.arange(OUT_SAMPLES)[None, :], OUT_SAMPLES)
    backward = np.stack([np.cos(angle), -np.sin(angle)])
    spread = np.zeros((2, BINS, 4, 4, OUT_SAMPLES), np.float32)
    for p in range(4):
        spread[:, :, p, p] = backward
    spread = spread.reshape(2, BINS * 4, 4 * OUT_SAMPLES)
    return [jnp.asarray(t, jnp.bfloat16) for t in (forward, twiddle, spread)]


def dot_nt(a, b):
    return lax.dot_general(a, b, (((1,), (1,)), ((), ())), preferred_element_type=jnp.float32)


def dot(a, b):
    return jnp.dot(a, b, preferred_element_type=jnp.float32)


def kernel(
    samples_hbm, steps_hbm, delay_hbm, forward_hbm, twiddle_hbm, spread_hbm, out_ref,
    samp, steps, delay, forward, twiddle, spread, tab, tabs, plain, send, recv, pick,
    ded, ded_in, rows, in_sem, const_sem, tab_send, tab_recv, spec_send, spec_recv, ded_send, ded_recv,
):
    me = lax.axis_index("chan")
    mx, my, mz = me // 16, me // 4 % 4, me % 4
    owner = jnp.where(mz < PLANES, 1, 0)
    rank = (me // 4) * PLANES + mz
    columns = {(x, y): (mx + x) % 2 * 16 + (my + y) % 4 * 4 for x, y in TURNS}

    small = [
        pltpu.make_async_copy(src, dst, const_sem.at[i])
        for i, (src, dst) in enumerate(
            (
                (steps_hbm, steps),
                (delay_hbm, delay),
                (forward_hbm, forward),
                (twiddle_hbm, twiddle),
                (spread_hbm, spread),
            )
        )
    ]
    loads = [
        pltpu.make_async_copy(samples_hbm.at[i], samp.at[i], in_sem.at[i]) for i in range(BEAMS)
    ]
    for copy in small[:3] + loads + small[3:]:
        copy.start()

    barrier = pltpu.get_barrier_semaphore()

    @pl.when(owner == 1)
    def _():
        for peer in [columns[x, y] + z for x, y in TURNS for z in (3, 2, 1, 0)]:

            @pl.when(peer != me)
            def _():
                pl.semaphore_signal(barrier, inc=1, device_id={"chan": peer}, device_id_type=MESH)

    small[0].wait()
    small[1].wait()
    tab[0:1, :] = delay[...]
    tab[1:2, :] = jnp.concatenate([steps[...]] * (CHAN_DEV // TRIAL_DEV), axis=1)
    small[2].wait()

    def spectrum(i):
        loads[2 * i].wait()
        loads[2 * i + 1].wait()
        block = samp[2 * i : 2 * i + 2].reshape(2 * CHAN_DEV, SAMPLES)
        product = dot_nt(forward[...], block)
        energy = jnp.zeros((2 * CHAN_DEV, 128), jnp.float32)
        for j in range(SAMPLES // 128):
            piece = block[:, 128 * j : 128 * (j + 1)].astype(jnp.float32)
            energy += piece * piece
        coarse = energy.astype(jnp.bfloat16)
        fine = (energy - coarse.astype(jnp.float32)).astype(jnp.bfloat16)
        energy = dot_nt(
            jnp.ones((8, 256), jnp.bfloat16), jnp.concatenate([coarse, fine], axis=1)
        )[0:1]
        scaling = 1.0 / jnp.sqrt(energy / SAMPLES + EPSILON) / math.sqrt(SAMPLES)
        product = product * scaling
        for half in range(2):
            for r in range(2):
                plain[pl.ds(r * BEAMS + 2 * i + half, BINS, stride=ROWS), :] = product[
                    r * BINS : (r + 1) * BINS, half * CHAN_DEV : (half + 1) * CHAN_DEV
                ]

    def post(src, dst, send_sem, recv_sem, peer):
        @pl.when(peer != me)
        def _():
            pltpu.make_async_remote_copy(
                src_ref=src,
                dst_ref=dst,
                send_sem=send_sem,
                recv_sem=recv_sem,
                device_id={"chan": peer},
                device_id_type=MESH,
            ).start()

    def keep(src, dst, sem):
        pltpu.make_async_copy(src, dst, sem).start()

    def arrived(part, sem):
        pltpu.make_async_copy(part, part, sem).wait()

    slot = me % 16
    for i in range(3):
        spectrum(i)
    pl.semaphore_wait(barrier, OWNERS - owner)
    for x, y, z in TO_OWNERS:
        peer = columns[x, y] + z
        post(tab, tabs.at[me], tab_send, tab_recv.at[slot], peer)

    @pl.when(owner == 1)
    def _():
        keep(tab, tabs.at[me], tab_recv.at[slot])

    spectrum(3)
    send[...] = plain[...].astype(jnp.bfloat16).reshape(BINS, ROWS, CHAN_DEV)
    for x, y, z in TO_OWNERS:
        peer = columns[x, y] + z
        first = (columns[x, y] // 4 * PLANES + z) * OWNED
        post(send.at[pl.ds(first, OWNED)], recv.at[me], spec_send, spec_recv.at[slot], peer)

    def dedisperse():
        low_iota = lax.broadcasted_iota(jnp.int32, (LOW, CHAN_DEV), 0).astype(jnp.float32).astype(jnp.bfloat16)
        one = jnp.ones((), jnp.bfloat16)
        zero = jnp.zeros((), jnp.bfloat16)

        def hot(index):
            row = jnp.broadcast_to(index.astype(jnp.float32), (16, CHAN_DEV)).astype(jnp.bfloat16)
            return jnp.where(low_iota == jnp.concatenate([row] * (LOW // 16), axis=0), one, zero)

        def binning(pairs):
            left, right = [], []
            for y, z in pairs:
                arrived(recv.at[pl.ds(0, 2)], spec_recv.at[4 * y + z])
            for y, z in pairs:
                for x in range(2):
                    src = chan_of(x, y, z)
                    place = tabs[src, 0:1, :]
                    right.append(hot(place % LOW))
                    high = jnp.broadcast_to(place // LOW % QUARTERS, (ROWS, CHAN_DEV))
                    masks = [
                        jnp.where(high == q, 1.0, 0.0).astype(jnp.bfloat16) for q in range(QUARTERS)
                    ]
                    left.append(
                        jnp.concatenate(
                            [recv[src, k] * masks[q] for k in range(OWNED) for q in range(QUARTERS)],
                            axis=0,
                        )
                    )
            return dot_nt(jnp.concatenate(left, axis=1), jnp.concatenate(right, axis=1))

        def placed(y, z):
            arrived(tabs.at[pl.ds(0, 2)], tab_recv.at[4 * y + z])

        for y, z in PAIRS:
            placed(y, z)
        lane = lax.broadcasted_iota(jnp.int32, (1, 128), 1)
        turns = [[] for _ in range(OWNED)]
        for g in range(8):
            step = tabs[4 * g + 3, 1:2, :]
            for q in range(3):
                step = jnp.where(lane // TRIAL_DEV == q, tabs[4 * g + q, 1:2, :], step)
            for k in range(OWNED):
                m = step * (rank * OWNED + k + 1) % SAMPLES
                turns[k].append(m % QUARTERS)
                pick[k, :, g * 128 : (g + 1) * 128] = hot(m // QUARTERS)
        small[3].wait()
        binned = binning(PAIRS)

        parts = []
        for q in range(QUARTERS):
            stack = []
            for k in range(OWNED):
                base = k * QUARTERS * ROWS
                re = [binned[base + ROWS * j : base + ROWS * j + 8] for j in range(QUARTERS)]
                im = [binned[base + ROWS * j + 8 : base + ROWS * j + 16] for j in range(QUARTERS)]
                if q == 0:
                    pair = (re[0] + re[1] + re[2] + re[3], im[0] + im[1] + im[2] + im[3])
                elif q == 1:
                    pair = (re[0] - im[1] - re[2] + im[3], im[0] + re[1] - im[2] - re[3])
                elif q == 2:
                    pair = (re[0] - re[1] + re[2] - re[3], im[0] - im[1] + im[2] - im[3])
                else:
                    pair = (re[0] + im[1] - re[2] - im[3], im[0] - re[1] - im[2] + re[3])
                pair = jnp.concatenate(pair, axis=0)
                coarse = pair.astype(jnp.bfloat16)
                stack += [coarse, (pair - coarse.astype(jnp.float32)).astype(jnp.bfloat16)]
            turned = dot(jnp.concatenate(stack, axis=0), twiddle[q])
            parts.append([])
            for k in range(OWNED):
                both = turned[32 * k : 32 * k + 16] + turned[32 * k + 16 : 32 * k + 32]
                real = both[0:8, :LOW] - both[8:16, LOW:]
                imag = both[0:8, LOW:] + both[8:16, :LOW]
                both = jnp.concatenate([real, imag], axis=0) / math.sqrt(CHANNELS)
                parts[q].append(both.astype(jnp.bfloat16))

        sub = lax.broadcasted_iota(jnp.int32, (8, 128), 0)
        lanes = lax.broadcasted_iota(jnp.int32, (8, 128), 1)
        left = lanes < 64
        even = lanes % 64 < 32
        stay = (sub < 4) == even
        for k in range(OWNED):
            table = jnp.concatenate([parts[q][k] for q in range(QUARTERS)], axis=0)
            picked = dot(table, pick[k])
            for g in range(8):
                halves = []
                for r in range(2):
                    chosen = None
                    for q in range(QUARTERS):
                        at = q * ROWS + r * 8
                        value = picked[at : at + 8, g * 128 : (g + 1) * 128]
                        chosen = value if q == 0 else jnp.where(turns[k][g] == q, value, chosen)
                    halves.append(chosen)
                a, b = halves
                mixed = (
                    jnp.where(left, a, pltpu.roll(b, 64, 1)),
                    jnp.where(left, pltpu.roll(a, 64, 1), b),
                )
                for pair in range(2):
                    v = mixed[pair]
                    swap = jnp.where(even, pltpu.roll(v, 96, 1), pltpu.roll(v, 32, 1))
                    v = jnp.where(stay, v, pltpu.roll(swap, 4, 0)).astype(jnp.bfloat16)
                    ded[4 * g + 2 * pair, k] = v[0:4]
                    ded[4 * g + 2 * pair + 1, k] = v[4:8]

    own = pl.ds(rank * OWNED, OWNED)

    @pl.when(owner == 1)
    def _():
        keep(send.at[own], recv.at[me], spec_recv.at[slot])
        dedisperse()
        for x, y, z in TO_ALL:
            peer = columns[x, y] + z
            post(ded.at[peer], ded_in.at[own], ded_send, ded_recv, peer)
        keep(ded.at[me], ded_in.at[own], ded_recv)
        arrived(tabs.at[pl.ds(0, OWNERS - 1)], tab_send)
        arrived(recv.at[pl.ds(0, OWNERS - 1)], spec_send)

    @pl.when(owner == 0)
    def _():
        small[3].wait()
        arrived(tabs.at[pl.ds(0, OWNERS)], tab_send)
        arrived(recv.at[pl.ds(0, OWNERS)], spec_send)

    small[4].wait()
    arrived(ded_in, ded_recv)
    for src in range(GROUPS):
        rows[4 * src : 4 * src + 4] = ded_in[src].astype(jnp.float32)
    moved = rows[...].T.astype(jnp.bfloat16)
    series = dot(moved[0:64], spread[0]) + dot(moved[64:128], spread[1])
    series = series / math.sqrt(BINS)
    for high in range(2):
        for p in range(4):
            out_ref[4 * high + p] = series[32 * high : 32 * high + 32, 128 * p : 128 * (p + 1)]

    @pl.when(owner == 1)
    def _():
        arrived(ded.at[pl.ds(0, GROUPS - 1)], ded_send)


def per_device(samples, trial_steps, chan_delay):
    forward, twiddle, spread = tables()
    hbm = pl.BlockSpec(memory_space=pltpu.HBM)
    bf16, f32, i32 = jnp.bfloat16, jnp.float32, jnp.int32
    dma = pltpu.SemaphoreType.DMA
    return pl.pallas_call(
        kernel,
        out_shape=pltpu.VMEM((BEAMS, TRIAL_DEV, OUT_SAMPLES), f32),
        in_specs=[hbm] * 6,
        out_specs=pl.BlockSpec(memory_space=pltpu.VMEM),
        scratch_shapes=[
            pltpu.VMEM((BEAMS, CHAN_DEV, SAMPLES), bf16),
            pltpu.VMEM((1, TRIAL_DEV), i32),
            pltpu.VMEM((1, CHAN_DEV), i32),
            pltpu.VMEM((2 * BINS, SAMPLES), bf16),
            pltpu.VMEM((QUARTERS, LOW, 2 * LOW), bf16),
            pltpu.VMEM((2, 4 * BINS, 4 * OUT_SAMPLES), bf16),
            pltpu.VMEM((2, CHAN_DEV), i32),
            pltpu.VMEM((GROUPS, 2, CHAN_DEV), i32),
            pltpu.VMEM((BINS * ROWS, CHAN_DEV), f32),
            pltpu.VMEM((BINS, ROWS, CHAN_DEV), bf16),
            pltpu.VMEM((GROUPS, OWNED, ROWS, CHAN_DEV), bf16),
            pltpu.VMEM((OWNED, LOW, TRIALS), bf16),
            pltpu.VMEM((GROUPS, OWNED, 4, 128), bf16),
            pltpu.VMEM((BINS, 4, 128), bf16),
            pltpu.VMEM((GROUPS * 4, 128), f32),
            dma((BEAMS,)),
            dma((5,)),
            dma(()),
            dma((len(PAIRS),)),
            dma(()),
            dma((len(PAIRS),)),
            dma(()),
            dma(()),
        ],
        compiler_params=pltpu.CompilerParams(collective_id=0, has_side_effects=True),
    )(
        samples,
        trial_steps.reshape(1, TRIAL_DEV),
        chan_delay.reshape(1, CHAN_DEV),
        forward,
        twiddle,
        spread,
    )


def solution(mesh):
    in_specs = (P("beam", "chan", None), P("chan"), P("chan"))
    out_specs = P("beam", "chan", None)
    return jax.shard_map(
        per_device, mesh=mesh, in_specs=in_specs, out_specs=out_specs, check_vma=False
    )
```
